32 devices in a mesh: row: 4 (over x, core), col: 2 (over y), layer: 4 (over z).
Axes of the slice: x: 2, y: 2, z: 4, core: 2. Of those that a mesh axis runs over, the one named last changes fastest.
Arguments:
- density_matrix: bfloat16 [2048, 2048], P('row', 'col'), may hold values from -3 to 3
- block_mask: int32 [32, 32], P('row', 'col'), may hold values 0 or 1
- intersection_weights: float32 [2048], P(('col', 'layer')), may hold values from -0.125 to 0.125
- exponents: float32 [2048], P('row'), may hold values from 0.5 to 8
- anchor_x: int32 [32], P('row'), may hold values from 0 to 31
- anchor_y: int32 [32], P('row'), may hold values from 0 to 127, as said below
- anchor_z: int32 [32], P('row'), may hold values from 0 to 127
Outputs:
- squared: bfloat16 [2048, 2048], P('row', ('col', 'layer'))
- density: float32 [128, 128, 128], P('row', ('col', 'layer'))
The draws below stay inside these ranges and needn't reach their ends.
Inputs may be any that keep to these rules, and one draw needn't show every extreme that they name: `anchor_y`: block row a starts in the second dimension between (a mod (8)) * 16 and that plus 16 - 1.
All inputs are finite; a program needn't handle non-finite values. No bound on the sum of `block_mask` on one device may be relied on, other than what follows from the above.
Results may differ from the reference program's by a relative error of at most 0.0055.
Values may be sent and summed in bfloat16 or wider, within the bound.
A program may use at most 64 MiB of HBM per device.

```python
import math
import jax
import jax.numpy as jnp
from jax import lax

BLOCK = 64
TILE = 16
APR = 8
SX = 32
SY = 16
GZ = 128
NATOMS = 32
M = 2048
GX = 128
GY = 128


def draw_anchor_y(key, part):
    slab_count = GY // SY
    atom_ids = jnp.arange(NATOMS, dtype=jnp.int32)
    within = jax.random.randint(jax.random.fold_in(key, 11), (NATOMS,), 0, SY, dtype=jnp.int32)
    within = jnp.where(atom_ids == 0, 0, within)
    within = jnp.where(atom_ids == NATOMS - 1, SY - 1, within)
    return (atom_ids % slab_count * SY + within).astype(jnp.int32)


def set_ends(values, rng, smallest, largest):
    longest = values.shape.index(max(values.shape))
    spots = []
    for shift in (0, 1):
        where = [jax.random.randint(jax.random.fold_in(rng, axis), (), 0, length) for axis, length in enumerate(values.shape)]
        where[longest] = (where[longest] + shift) % values.shape[longest]
        spots.append(tuple(where))
    return values.at[spots[0]].set(smallest).at[spots[1]].set(largest)


def steps_of(key, extent, split, smallest, top_value):
    def one(dim, parts):
        draws = jax.random.uniform(jax.random.fold_in(jax.random.fold_in(key, 6), dim), (parts,), jnp.float32, smallest / len(split), top_value / len(split))
        return jnp.repeat(jnp.exp(draws), extent[dim] // parts).reshape((-1,) + (1,) * (len(extent) - dim - 1))

    factor_of = one(*split[0])
    for cut in split[1:]:
        factor_of = factor_of * one(*cut)
    return factor_of


def bell_draw(rng, dims, width, bound, pieces=(), kind=jnp.bfloat16):
    values = jax.random.normal(rng, dims, jnp.float32) * width
    if len(pieces) > 0:
        values = steps_of(rng, dims, pieces, -0.22, 0.18) * values
    return jnp.clip(values, min=-bound, max=bound).astype(kind)


def setup_inputs(seed: int = 0) -> dict:
    keys = jax.random.split(jax.random.key(seed), 8)
    return {
        "density_matrix": bell_draw(keys[0], (M, M), (1.414 / M ** 0.25), 3.0, ((0, 4), (1, 2))),
        "block_mask": set_ends((jax.random.randint(keys[1], (NATOMS, NATOMS), 0, 2) < 1).astype(jnp.int32), jax.random.fold_in(keys[1], 1), 0, 1),
        "intersection_weights": bell_draw(keys[2], (M,), M ** -0.5, 0.125, ((0, 8),), jnp.float32),
        "exponents": jnp.clip(jnp.exp(math.log(8.0) - 2.7725887 * jax.random.uniform(keys[3], (M,), jnp.float32) ** steps_of(keys[3], (M,), ((0, 4),), -0.2, 0.2)), 0.5, 8.0),
        "anchor_x": set_ends(jax.random.randint(keys[4], (NATOMS,), 0, SX), jax.random.fold_in(keys[4], 1), 0, SX - 1).astype(jnp.int32),
        "anchor_y": draw_anchor_y(jax.random.fold_in(keys[7], 71), 0),
        "anchor_z": set_ends(jax.random.randint(keys[6], (NATOMS,), 0, GZ), jax.random.fold_in(keys[6], 1), 0, GZ - 1).astype(jnp.int32),
    }


grid_step_sq = 0.0625


def reference(density_matrix, block_mask, intersection_weights, exponents, anchor_x, anchor_y, anchor_z):
    wide_mask = jnp.repeat(jnp.repeat(block_mask, BLOCK, 0), BLOCK, 1)
    masked = jnp.where(wide_mask > 0, density_matrix, jnp.zeros_like(density_matrix))
    product = jnp.dot(masked, masked, preferred_element_type=jnp.float32)
    squared = product.astype(jnp.bfloat16)
    charges = jnp.dot(product, intersection_weights, precision=lax.Precision.HIGHEST)
    offsets = jnp.arange(TILE, dtype=jnp.int32)
    centre = offsets.astype(jnp.float32) - 7.5

    def deposit(atom_at, grid_now):
        atom_charges = lax.dynamic_slice_in_dim(charges, atom_at * BLOCK, BLOCK)
        decay_rates = lax.dynamic_slice_in_dim(exponents, atom_at * BLOCK, BLOCK)
        profile = jnp.exp(-decay_rates[:, None] * grid_step_sq * centre[None, :] ** 2)
        tile_values = jnp.einsum("k,kx,ky,kz->xyz", atom_charges, profile, profile, profile, precision=lax.Precision.HIGHEST)
        x_cells = ((atom_at // APR) * SX + anchor_x[atom_at] + offsets) % GX
        y_cells = (anchor_y[atom_at] + offsets) % GY
        z_cells = (anchor_z[atom_at] + offsets) % GZ
        return grid_now.at[x_cells[:, None, None], y_cells[None, :, None], z_cells[None, None, :]].add(tile_values)

    density = lax.fori_loop(0, NATOMS, deposit, jnp.zeros((GX, GY, GZ), jnp.float32))
    return squared, density
```

```python
import functools

import jax
import jax.numpy as jnp
from jax import lax
from jax.experimental import pallas as pl
from jax.experimental.pallas import tpu as pltpu
from jax.sharding import PartitionSpec as P

BLOCK = 64
TILE = 16
SX = 32
SY = 16
GZ = 128
STEP_SQ = 0.0625
MESH = pl.DeviceIdType.MESH
F32 = jnp.float32
BF16 = jnp.bfloat16
LANES = 128
OUT_CHUNKS = 2
LOADS = 2
SUB = 2
EARLY = 2
CHARGE_AT = 1
DETOUR = (1, 0, 0, 0)


def dot_nt(a, b):
    return lax.dot_general(a, b, (((1,), (1,)), ((), ())), preferred_element_type=F32)


def hi_lo(x):
    high = x.astype(BF16).astype(F32)
    return jnp.concatenate([high, x - high], axis=0).astype(BF16)


def kernel(
    sizes,
    a_hbm, mask_hbm, w_hbm, e_hbm, ax_hbm, ay_hbm, az_hbm,
    sq_ref, den_ref,
    a_ref, mask_ref, w_ref, e_ref, ax_ref, ay_ref, az_ref, load_sem,
    m_buf, mine, wide, right, own_part, part_out, part_in, detour,
    v_out, v_all, q_out, q_all, pack, pack_in, shape_xy, shape_low, shape_z,
    piece_send, piece_recv, fwd_send, relay_send, own_sem, part_send, part_recv, detour_recv, detour_send,
    v_send, v_recv, q_send, q_recv, pack_send, pack_recv, ready, below, above,
):
    nr, nc, nl = sizes
    ratio = nr // nc
    square = nr == 4 and nc == 2
    rows, cols = a_ref.shape
    width = cols // nl
    atoms = rows // BLOCK
    r, c, l = lax.axis_index("row"), lax.axis_index("col"), lax.axis_index("layer")
    sibling = r + 1 - 2 * (r % 2)
    following = (r + 1) % nr
    home = r // ratio
    slot = r % ratio
    at_home = home == c
    away = jnp.logical_not(at_home)
    across = (r + 2) % nr
    other = (c + 1) % nc

    def remote(src, dst, send, recv, device):
        return pltpu.make_async_remote_copy(
            src_ref=src, dst_ref=dst, send_sem=send, recv_sem=recv,
            device_id=device, device_id_type=MESH,
        )

    def signal(sem, device):
        pl.semaphore_signal(sem, inc=1, device_id=device, device_id_type=MESH)

    chunks = width // LANES
    tall = rows // LOADS
    part_rows = rows // SUB
    small = [
        pltpu.make_async_copy(src, dst, load_sem.at[at])
        for at, (src, dst) in enumerate((
            (mask_hbm, mask_ref), (w_hbm, w_ref), (e_hbm, e_ref),
            (ax_hbm, ax_ref), (ay_hbm, ay_ref), (az_hbm, az_ref),
        ))
    ]
    large = [
        pltpu.make_async_copy(
            a_hbm.at[pl.ds(p * tall, tall), :], a_ref.at[pl.ds(p * tall, tall), :], load_sem.at[6 + p]
        )
        for p in range(LOADS)
    ]

    barrier = pltpu.get_barrier_semaphore()
    if square:
        peers = [(dr, 0, 0) for dr in range(1, nr)]
        for dr in (0, 1):
            signal(barrier, ((r // 2) * 2 + (r + dr) % 2, other, l))
        n_peers = 2
    else:
        peers = [
            (dr, dc, dl) for dr in range(nr) for dc in range(nc) for dl in range(nl)
            if (dr or dc or dl) and (dl == 0 or dr in (0, 1, nr - 1))
        ]
        n_peers = 0
    for dr, dc, dl in peers:
        signal(barrier, ((r + dr) % nr, (c + dc) % nc, (l + dl) % nl))
    n_peers += len(peers)
    has_above = l + 1 < nl
    has_below = l > 0

    def to_layers(up, down):
        @pl.when(has_above)
        def _():
            signal(up, (r, c, l + 1))

        @pl.when(has_below)
        def _():
            signal(down, (r, c, l - 1))

    if square:
        to_layers(barrier, barrier)
    for copy in small + large:
        copy.start()

    for copy in small:
        copy.wait()
    kept = jnp.where(mask_ref[...] > 0, 1.0, 0.0).astype(F32)
    spread = lax.broadcasted_iota(jnp.int32, (cols // BLOCK, cols), 1) // BLOCK
    pick = lax.broadcasted_iota(jnp.int32, (cols // BLOCK, cols), 0)
    wide[...] = jnp.dot(kept, jnp.where(spread == pick, 1.0, 0.0).astype(F32), preferred_element_type=F32)
    strip = pl.ds(pl.multiple_of(l * width, LANES), width)
    for b in range(atoms):
        if b % (atoms // LOADS) == 0:
            large[b // (atoms // LOADS)].wait()
        at = pl.ds(b * BLOCK, BLOCK)
        mine[at, :] = a_ref[at, strip] * jnp.broadcast_to(wide[b : b + 1, strip], (BLOCK, width)).astype(BF16)

    def squash(total):
        return total[0:1, :] + total[8:9, :]

    v_out[...] = squash(dot_nt(hi_lo(jnp.broadcast_to(w_ref[...], (8, width))), mine[...]))

    if square:
        n_peers = n_peers + has_above.astype(jnp.int32) + has_below.astype(jnp.int32)
    pl.semaphore_wait(barrier, n_peers)
    if square:
        signal(ready.at[0], (across, c, l))

    def v_copy(k):
        return remote(
            v_out, v_all.at[slot, c], v_send.at[k], v_recv.at[slot * nc + c], ((r + k) % nr, home, l)
        )

    def mine_at(h, s):
        return mine.at[pl.ds(s * part_rows, part_rows), pl.ds(h * LANES, LANES)]

    def piece(i, cc, h, s):
        return right.at[i, cc, h, pl.ds(s * part_rows, part_rows), :]

    def sem_at(i, cc, h, s):
        return ((i * nc + cc) * chunks + h) * SUB + s

    def piece_copy(k, h, s):
        return remote(
            mine_at(h, s), piece(slot, c, h, s), piece_send.at[(k * chunks + h) * SUB + s],
            piece_recv.at[sem_at(slot, c, h, s)], ((r + 2 * k) % nr, home, l),
        )

    def own_copy(h, s):
        return pltpu.make_async_copy(mine_at(h, s), piece(slot, c, h, s), own_sem.at[h * SUB + s])

    def own_fwd(h, s):
        return remote(
            mine_at(h, s), piece(slot, c, h, s), fwd_send.at[sem_at(slot, c, h, s)],
            piece_recv.at[sem_at(slot, c, h, s)], (sibling, c, l),
        )

    def fwd_copy(i, cc, h, s):
        return remote(
            piece(i, cc, h, s), piece(i, cc, h, s), fwd_send.at[sem_at(i, cc, h, s)],
            piece_recv.at[sem_at(i, cc, h, s)], (sibling, c, l),
        )

    def relay_copy(h, s):
        return remote(
            piece(slot, other, h, s), piece(slot, other, h, s), relay_send.at[h * SUB + s],
            piece_recv.at[sem_at(slot, other, h, s)], (across, c, l),
        )

    def landed(i, cc, h, s):
        fwd_copy(i, cc, h, s).wait_recv()

    units = [(h, s) for h in range(chunks) for s in range(SUB)]
    relayed = [u for u in units if square and u[0] == chunks - 1]
    straight = [u for u in units if u not in relayed]
    order = relayed + straight

    @pl.when(at_home)
    def _():
        v_all[slot, c] = v_out[...]
        for k in range(1, nr):
            v_copy(k).start()
        for h, s in units:
            own_copy(h, s).start()
        for h, s in units:
            own_fwd(h, s).start()
        if not square:
            for h, s in units:
                for k in range(1, nr // 2):
                    piece_copy(k, h, s).start()
        else:
            for h, s in order[:EARLY]:
                piece_copy(1, h, s).start()

    if square:
        near = (r // 2) * 2

        @pl.when(away)
        def _():
            v_copy(0).start()

            @pl.when(slot == 0)
            def _():
                v_copy(1).start()

            @pl.when(slot == 1)
            def _():
                v_copy(3).start()

            for h, s in order:
                piece_copy(0, h, s).start()
    else:
        @pl.when(away)
        def _():
            for k in range(nr):
                v_copy(k).start()
            for h, s in units:
                for k in range(nr // 2):
                    piece_copy(k, h, s).start()

    lane_atom = lax.broadcasted_iota(jnp.int32, (8, rows), 1) // BLOCK
    sub = lax.broadcasted_iota(jnp.int32, (8, rows), 0)
    table = jnp.broadcast_to(e_ref[...], (8, rows))
    for j in range(atoms):
        here = lane_atom == j
        for at, ref in ((1, ax_ref), (2, ay_ref), (3, az_ref)):
            table = jnp.where(here & (sub == at), ref[j].astype(F32), table)
    pack[...] = table
    pack_copy = remote(pack, pack_in, pack_send.at[0], pack_recv.at[0], (following, c, l))
    pack_copy.start()

    for b in range(atoms):
        at = pl.ds(b * BLOCK, BLOCK)
        m_buf[at, :] = a_ref[at, :] * jnp.broadcast_to(wide[b : b + 1, :], (BLOCK, cols)).astype(BF16)

    if square:
        pl.semaphore_wait(ready.at[0], 1)

        @pl.when(away)
        def _():
            v_copy(2).start()

            @pl.when(slot == 0)
            def _():
                v_copy(3).start()

            @pl.when(slot == 1)
            def _():
                v_copy(1).start()

            for h, s in straight:
                piece_copy(1, h, s).start()

        to_layers(below.at[0], above.at[0])

    def layer_step(at):
        @pl.when(has_above)
        def _():
            pl.semaphore_wait(above.at[at], 1)

        @pl.when(has_below)
        def _():
            pl.semaphore_wait(below.at[at], 1)

        if at + 1 < nl - 1:
            to_layers(below.at[at + 1], above.at[at + 1])

    y_first = (c * nl + l) * SY
    y_count = nc * nl * SY

    def profiles(g, ref):
        rate = ref[0:1, :] * (-STEP_SQ)

        def profile(t):
            value = jnp.exp(rate * (t - 7.5) * (t - 7.5))
            return jnp.where((t >= 0.0) & (t < float(TILE)), value, 0.0)

        tx = lax.broadcasted_iota(jnp.int32, (SX, rows), 0).astype(F32) + float(g * SX) - ref[1:2, :]
        ty = (lax.broadcasted_iota(jnp.int32, (SY, rows), 0) + y_first).astype(F32) - ref[2:3, :]
        ty = jnp.where(ty < 0.0, ty + float(y_count), ty)
        tz = lax.broadcasted_iota(jnp.int32, (GZ, rows), 0).astype(F32) - ref[3:4, :]
        tz = jnp.where(tz < 0.0, tz + float(GZ), tz)
        px, py = profile(tx), profile(ty)
        for x in range(SX):
            plane = px[x : x + 1, :] * py
            high = plane.astype(BF16)
            shape_xy[g, x * SY : (x + 1) * SY, :] = high
            shape_low[g, x * SY : (x + 1) * SY, :] = (plane - high.astype(F32)).astype(BF16)
        shape_z[g] = profile(tz)

    profiles(0, pack)
    if square:
        layer_step(0)

    def direct(i):
        return (c * ratio + i) % 2 == r % 2

    def pass_on(h, s, ks):
        for k in ks:
            cc = (c + k) % nc
            for i in range(ratio):

                @pl.when(direct(i) & jnp.logical_not((c * ratio + i == r) & (cc == c)))
                def _():
                    landed(i, cc, h, s)
                    fwd_copy(i, cc, h, s).start()

    def turn(j):
        if not square:
            return j
        return jnp.where(at_home, (j + 1) % chunks, j)

    def take(cc, h):
        for s in range(SUB):
            for i in range(ratio):

                @pl.when(jnp.logical_not(direct(i)))
                def _():
                    landed(i, cc, h, s)

    low = rows // OUT_CHUNKS

    def product(cc, h, at):
        total = jnp.dot(m_buf[at, 0:rows], right[0, cc, h], preferred_element_type=F32)
        for i in range(1, ratio):
            total = total + jnp.dot(
                m_buf[at, i * rows : (i + 1) * rows], right[i, cc, h], preferred_element_type=F32
            )
        return total

    outs = [(h, o) for h in range(chunks) for o in range(OUT_CHUNKS)]
    bent = [u for u in outs if square and DETOUR[u[0] * OUT_CHUNKS + u[1]]]

    def part_index(k, h, o):
        return ((k - 1) * chunks + h) * OUT_CHUNKS + o

    def part_copy(k, h, o):
        at = pl.ds(o * low, low)
        index = part_index(k, h, o)
        return remote(
            part_out.at[k - 1, h, at, :], part_in.at[k - 1, h, at, :], part_send.at[index],
            part_recv.at[index], (r, (c + k) % nc, l),
        )

    def bend_copy(h, o):
        at = pl.ds(o * low, low)
        return remote(
            part_out.at[0, h, at, :], detour.at[bent.index((h, o))], part_send.at[part_index(1, h, o)],
            detour_recv.at[bent.index((h, o))], (across, other, l),
        )

    def unbend_copy(h, o):
        at = pl.ds(o * low, low)
        return remote(
            detour.at[bent.index((h, o))], part_in.at[0, h, at, :], detour_send.at[bent.index((h, o))],
            part_recv.at[part_index(1, h, o)], (across, c, l),
        )

    def parts(j):
        h = turn(j)
        for k in range(1, nc):
            take((c + k) % nc, h)
            for o in range(OUT_CHUNKS):
                at = pl.ds(o * low, low)
                part_out[k - 1, h, at, :] = product((c + k) % nc, h, at).astype(BF16)
                if (j, o) in bent:

                    @pl.when(at_home)
                    def _():
                        part_copy(k, h, o).start()

                    @pl.when(away)
                    def _():
                        bend_copy(j, o).start()

                else:
                    part_copy(k, h, o).start()

    def unbend():
        @pl.when(away)
        def _():
            for h, o in bent:
                bend_copy(h, o).wait_recv()
                unbend_copy(h, o).start()

    def charge_share():
        for i in range(ratio):
            for cc in range(nc):

                @pl.when(jnp.logical_not((c * ratio + i == r) & (cc == c)))
                def _():
                    remote(
                        v_out, v_all.at[i, cc], v_send.at[0], v_recv.at[i * nc + cc], (sibling, c, l)
                    ).wait_recv()

        total = jnp.zeros((16, rows), F32)
        for i in range(ratio):
            v = v_all[i, 0]
            for cc in range(1, nc):
                v = v + v_all[i, cc]
            total = total + dot_nt(hi_lo(jnp.broadcast_to(v, (8, rows))), m_buf[:, i * rows : (i + 1) * rows])
        q_out[...] = squash(total)
        q_all[0, c, l] = q_out[...]

    def q_copy(g, k, m):
        index = (g * nc + k) * nl + m
        return remote(
            q_out, q_all.at[g, c, l], q_send.at[index], q_recv.at[index],
            ((r + g) % nr, (c + k) % nc, (l + m) % nl),
        )

    sent_q = [(g, k, m) for m in reversed(range(nl)) for g in range(2) for k in range(nc) if g or k or m]

    def own_late():
        if square:

            @pl.when(at_home)
            def _():
                for h, s in order[EARLY:]:
                    piece_copy(1, h, s).start()

    def charges():
        if square:
            layer_step(1)
        charge_share()
        if square:
            for at in range(2, nl - 1):
                layer_step(at)
        for g, k, m in sent_q:
            q_copy(g, k, m).start()

    if CHARGE_AT == 0:
        charges()
    for j in range(chunks):
        for s in range(SUB):
            pass_on(turn(j), s, range(1, nc))
            if square and j == 0:

                @pl.when(at_home)
                def _():
                    relay_copy(turn(j), s).start()

        if j == 0:
            own_late()
            if CHARGE_AT == 1:
                charges()
        parts(j)
        if j == 0:
            if CHARGE_AT == 2:
                charges()
            pack_copy.wait_recv()
            profiles(1, pack_in)
    unbend()
    for h, s in units:
        pass_on(h, s, (0,))

    @pl.when(at_home)
    def _():
        for h, s in units:
            own_copy(h, s).wait()

    for h in range(chunks):
        take(c, h)
        for o in range(OUT_CHUNKS):
            at = pl.ds(o * low, low)
            own_part[h, at, :] = product(c, h, at)

    for g, k, m in sent_q:
        q_copy(g, k, m).wait_recv()
    total = jnp.zeros((SX * SY, GZ), F32)
    for g in range(2):
        charge = jnp.zeros((1, rows), F32)
        for cc in range(nc):
            for ll in range(nl):
                charge = charge + q_all[g, cc, ll]
        value = shape_z[g] * charge
        high = value.astype(BF16)
        rest = (value - high.astype(F32)).astype(BF16)
        total = total + dot_nt(shape_xy[g], high) + dot_nt(shape_xy[g], rest) + dot_nt(shape_low[g], high)
    den_ref[...] = total.reshape(SX, SY, GZ)

    for h in range(chunks):
        for o in range(OUT_CHUNKS):
            at = pl.ds(o * low, low)
            total = own_part[h, at, :]
            for k in range(1, nc):
                part_copy(k, h, o).wait_recv()
                total = total + part_in[k - 1, h, at, :].astype(F32)
            sq_ref[at, h * LANES : (h + 1) * LANES] = total.astype(BF16)

    pack_copy.wait_send()
    for g, k, m in sent_q:
        q_copy(g, k, m).wait_send()
    for k in range(1, nr):
        v_copy(k).wait_send()
    for i in range(ratio):
        for cc in range(nc):

            @pl.when(direct(i))
            def _():
                for h, s in units:
                    fwd_copy(i, cc, h, s).wait_send()

    @pl.when(at_home)
    def _():
        for k in range(1, nr // 2):
            for h, s in units:
                piece_copy(k, h, s).wait_send()
        for h, s in relayed:
            relay_copy(h, s).wait_send()

    @pl.when(away)
    def _():
        v_copy(0).wait_send()
        for h, s in units:
            piece_copy(0, h, s).wait_send()
        for k in range(1, nr // 2):
            for h, s in straight:
                piece_copy(k, h, s).wait_send()
        for h, o in bent:
            unbend_copy(h, o).wait_send()

    for k in range(1, nc):
        for h, o in outs:
            part_copy(k, h, o).wait_send()


def store(sq_ref, den_ref, sq_out, den_out, sem):
    copies = [
        pltpu.make_async_copy(sq_ref, sq_out, sem.at[0]),
        pltpu.make_async_copy(den_ref, den_out, sem.at[1]),
    ]
    for copy in copies:
        copy.start()
    for copy in copies:
        copy.wait()


def local(sizes, density_matrix, block_mask, weights, exponents, anchor_x, anchor_y, anchor_z):
    nr, nc, nl = sizes
    ratio = nr // nc
    rows, cols = density_matrix.shape
    width = cols // nl
    dma = pltpu.SemaphoreType.DMA
    chunks = width // LANES
    pieces = ratio * nc * chunks
    outs = (nc - 1) * chunks * OUT_CHUNKS
    hbm = pl.BlockSpec(memory_space=pltpu.HBM)
    vmem = pl.BlockSpec(memory_space=pltpu.VMEM)
    inputs = (
        density_matrix, block_mask, weights.reshape(1, -1), exponents.reshape(1, -1),
        anchor_x, anchor_y, anchor_z,
    )
    shapes = (
        jax.ShapeDtypeStruct((rows, width), BF16),
        jax.ShapeDtypeStruct((SX, SY, GZ), F32),
    )
    results = pl.pallas_call(
        functools.partial(kernel, sizes),
        out_shape=(pltpu.VMEM((rows, width), BF16), pltpu.VMEM((SX, SY, GZ), F32)),
        in_specs=[hbm] * 7,
        out_specs=(vmem, vmem),
        scratch_shapes=[
            pltpu.VMEM((rows, cols), BF16),
            pltpu.VMEM(block_mask.shape, jnp.int32),
            pltpu.VMEM((1, width), F32),
            pltpu.VMEM((1, rows), F32),
            pltpu.SMEM(anchor_x.shape, jnp.int32),
            pltpu.SMEM(anchor_x.shape, jnp.int32),
            pltpu.SMEM(anchor_x.shape, jnp.int32),
            dma((6 + LOADS,)),
            pltpu.VMEM((rows, cols), BF16),
            pltpu.VMEM((rows, width), BF16),
            pltpu.VMEM((rows // BLOCK, cols), F32),
            pltpu.VMEM((ratio, nc, chunks, rows, LANES), BF16),
            pltpu.VMEM((chunks, rows, LANES), F32),
            pltpu.VMEM((nc - 1, chunks, rows, LANES), BF16),
            pltpu.VMEM((nc - 1, chunks, rows, LANES), BF16),
            pltpu.VMEM((len(DETOUR), rows // OUT_CHUNKS, LANES), BF16),
            pltpu.VMEM((1, rows), F32),
            pltpu.VMEM((ratio, nc, 1, rows), F32),
            pltpu.VMEM((1, rows), F32),
            pltpu.VMEM((2, nc, nl, 1, rows), F32),
            pltpu.VMEM((8, rows), F32),
            pltpu.VMEM((8, rows), F32),
            pltpu.VMEM((2, SX * SY, rows), BF16),
            pltpu.VMEM((2, SX * SY, rows), BF16),
            pltpu.VMEM((2, GZ, rows), F32),
            dma((nr // 2 * chunks * SUB,)),
            dma((pieces * SUB,)),
            dma((pieces * SUB,)),
            dma((chunks * SUB,)),
            dma((chunks * SUB,)),
            dma((outs,)),
            dma((outs,)),
            dma((len(DETOUR),)),
            dma((len(DETOUR),)),
            dma((nr,)),
            dma((ratio * nc,)),
            dma((2 * nc * nl,)),
            dma((2 * nc * nl,)),
            dma((1,)),
            dma((1,)),
            pltpu.SemaphoreType.REGULAR((1,)),
            pltpu.SemaphoreType.REGULAR((max(nl - 1, 1),)),
            pltpu.SemaphoreType.REGULAR((max(nl - 1, 1),)),
        ],
        compiler_params=pltpu.CompilerParams(
            collective_id=0, has_side_effects=True, vmem_limit_bytes=66_000_000
        ),
        name="square_collocate",
    )(*[pltpu.with_memory_space_constraint(x, pltpu.HBM) for x in inputs])
    return pl.pallas_call(
        store,
        out_shape=shapes,
        in_specs=[vmem] * 2,
        out_specs=(hbm, hbm),
        scratch_shapes=[dma((2,))],
        compiler_params=pltpu.CompilerParams(vmem_limit_bytes=4 * 1024 * 1024),
        name="store",
    )(*results)


def solution(mesh):
    sizes = (mesh.shape["row"], mesh.shape["col"], mesh.shape["layer"])
    return jax.shard_map(
        functools.partial(local, sizes),
        mesh=mesh,
        in_specs=(
            P("row", "col"), P("row", "col"), P(("col", "layer")),
            P("row"), P("row"), P("row"), P("row"),
        ),
        out_specs=(P("row", ("col", "layer")), P("row", ("col", "layer"), None)),
        check_vma=False,
    )
```
